32 devices in a mesh: node: 8 (over y, x, core), local: 4 (over z).
Axes of the slice: x: 2, y: 2, z: 4, core: 2. Of those that a mesh axis runs over, the one named last changes fastest.
Arguments:
- tokens: bfloat16 [4096, 4096], P(('node', 'local')), may hold values from -6 to 6
- grad_out: bfloat16 [4096, 4096], P(('node', 'local')), may hold values from -6 to 6
- router_logits: float32 [4096, 128], P(('node', 'local')), may hold values from -20 to 280
- group_id: int32 [4096], P(('node', 'local')), may hold values from 0 to 15, as said below
- expert_ids: int32 [4096, 2], P(('node', 'local')), may hold values from 0 to 7, as said below
- w_gate: bfloat16 [8, 4096, 1536], P('node', None, 'local'), may hold values from -0.09375 to 0.09375
- w_up: bfloat16 [8, 4096, 1536], P('node', None, 'local'), may hold values from -0.09375 to 0.09375
- w_down: bfloat16 [8, 1536, 4096], P('node', 'local'), may hold values from -0.15625 to 0.15625
Outputs:
- mixed: bfloat16 [4096, 4096], P(('node', 'local'))
- d_tokens: bfloat16 [4096, 4096], P(('node', 'local'))
- d_logits: float32 [4096, 128], P(('node', 'local'))
- grad_gate: bfloat16 [8, 4096, 1536], P('node', None, 'local')
- grad_up: bfloat16 [8, 4096, 1536], P('node', None, 'local')
- grad_down: bfloat16 [8, 1536, 4096], P('node', 'local')
The draws below stay inside these ranges and needn't reach their ends.
Inputs may be any that keep to these rules, and one draw needn't show every extreme that they name: `group_id`: A token is computed here when its group is below 1. Among the tokens of one device no expert of those groups is named by more than 6 tokens, and one such expert is named by exactly 6 tokens of every device. `expert_ids`: the two numbers of a token differ; both name experts of the token's group.
All inputs are finite; a program needn't handle non-finite values.
Results may differ from the reference program's by a relative error of at most 0.0065.
Values may be sent and summed in bfloat16 or wider, within the bound.
A program may use at most 192 MiB of HBM per device.

```python
import math
import jax
import jax.numpy as jnp
from jax import lax

D = 4096
F = 1536
GSIZE = 8
GROUPS_ALL = 16
LOGITS = 128
EXPERTS = 8
WGROUPS = 1
TOK_DEV = 128
CAP = 6
TOKENS = 4096


def routing_table(key):
    base_key = jax.random.fold_in(key, 7301)
    subkeys = jax.random.split(base_key, 8)
    block_count = TOKENS // TOK_DEV
    window_groups = EXPERTS // GSIZE
    window_pick = jax.random.randint(subkeys[0], (TOKENS,), 0, 2)
    inside_group = jax.random.randint(subkeys[1], (TOKENS,), 0, window_groups)
    outside_group = window_groups + jax.random.randint(subkeys[2], (TOKENS,), 0, GROUPS_ALL - window_groups)
    group_ids = jnp.where(window_pick == 0, inside_group, outside_group)
    first_draw = jax.random.randint(subkeys[3], (TOKENS,), 0, GSIZE)
    second_draw = jax.random.randint(subkeys[4], (TOKENS,), 0, GSIZE)
    relabel = jax.random.permutation(subkeys[5], GSIZE)
    first_expert = relabel[jnp.minimum(first_draw, second_draw)]
    offset_draw = jax.random.randint(subkeys[6], (TOKENS,), 1, GSIZE)
    hot_expert = jax.random.randint(subkeys[7], (), 0, EXPERTS)
    block_keys = jax.random.split(jax.random.fold_in(base_key, 11), block_count)
    block_ranks = jax.vmap(lambda single: jax.random.permutation(single, TOK_DEV))(block_keys)
    forced = (block_ranks < CAP).reshape(TOKENS)
    group_ids = jnp.where(forced, hot_expert // GSIZE, group_ids)
    first_expert = jnp.where(forced, hot_expert % GSIZE, first_expert)
    second_expert = (first_expert + offset_draw) % GSIZE
    pair_ids = jnp.stack([first_expert, second_expert], axis=1)
    inside = group_ids < window_groups
    target = jnp.where(inside[:, None], group_ids[:, None] * GSIZE + pair_ids, EXPERTS)
    expert_range = jnp.arange(EXPERTS, dtype=jnp.int32)
    onehot = (target[:, :, None] == expert_range[None, None, :]).astype(jnp.int32)
    per_token = jnp.sum(onehot, axis=1).reshape(block_count, TOK_DEV, EXPERTS)
    positions = jnp.arange(TOK_DEV, dtype=jnp.int32)[None, :]
    order_key = jnp.where(forced.reshape(block_count, TOK_DEV), 0, TOK_DEV) + positions
    order_index = jnp.argsort(order_key, axis=1, stable=True)
    ordered = jnp.take_along_axis(per_token, order_index[:, :, None], axis=1)
    earlier = jnp.cumsum(ordered, axis=1) - ordered
    inverse = jnp.argsort(order_index, axis=1, stable=True)
    rank_table = jnp.take_along_axis(earlier, inverse[:, :, None], axis=1).reshape(TOKENS, 1, EXPERTS)
    slot_rank = jnp.sum(onehot * rank_table, axis=2)
    over_cap = jnp.any(inside[:, None] & (slot_rank >= CAP), axis=1)
    group_ids = jnp.where(over_cap, outside_group, group_ids)
    return (group_ids.astype(jnp.int32), pair_ids.astype(jnp.int32))


def draw_group_id(key, part):
    return routing_table(key)[0]


def draw_expert_ids(key, part):
    return routing_table(key)[1]


def draw_router_logits(key, part):
    base_key = jax.random.fold_in(key, 4409)
    subkeys = jax.random.split(base_key, 6)
    group_ids = routing_table(key)[0]
    columns = jnp.arange(LOGITS, dtype=jnp.int32)
    member = (columns // GSIZE)[None, :] == group_ids[:, None]
    depth = jax.random.uniform(subkeys[5], (TOKENS, 1), jnp.float32, 9.0, 10.0)
    lowered = jnp.where(member, depth, 0.0)
    column_scale = jnp.exp(jax.random.uniform(subkeys[0], (LOGITS,), jnp.float32, math.log(0.5), math.log(0.8)))
    base_values = jnp.clip(jax.random.normal(subkeys[2], (TOKENS, LOGITS), jnp.float32) * column_scale[None, :], -12.0, 12.0)
    values = jnp.clip(base_values - lowered, -20.0, 20.0)
    return values.astype(jnp.float32)


def block_levels(own_key, dims, shards, smallest, high):
    def one(dim, parts):
        draws = jax.random.uniform(jax.random.fold_in(jax.random.fold_in(own_key, 6), dim), (parts,), jnp.float32, smallest / len(shards), high / len(shards))
        return jnp.repeat(jnp.exp(draws), dims[dim] // parts).reshape((-1,) + (1,) * (len(dims) - dim - 1))

    loudness = one(*shards[0])
    for cut in shards[1:]:
        loudness = loudness * one(*cut)
    return loudness


def scatter_about(key, shape, scale, reach, cuts=(), kind=jnp.bfloat16):
    array = scale * jax.random.normal(key, shape, jnp.float32)
    if cuts:
        array = array * block_levels(key, shape, cuts, -0.22, 0.18)
    return jnp.clip(array, -reach, reach).astype(kind)


def setup_inputs(seed: int = 0) -> dict:
    keys = jax.random.split(jax.random.key(seed), 9)
    tokens = scatter_about(keys[0], (TOKENS, D), 1.0, 6.0, ((0, 32),))
    grad_out = scatter_about(keys[1], (TOKENS, D), 1.0, 6.0, ((0, 32),))
    router_logits = draw_router_logits(jax.random.fold_in(keys[8], 71), 0)
    group_id = draw_group_id(jax.random.fold_in(keys[8], 71), 0)
    expert_ids = draw_expert_ids(jax.random.fold_in(keys[8], 71), 0)
    w_gate = scatter_about(keys[5], (EXPERTS, D, F), D ** -0.5, 0.09375, ((0, 8), (2, 4)))
    w_up = scatter_about(keys[6], (EXPERTS, D, F), D ** -0.5, 0.09375, ((0, 8), (2, 4)))
    w_down = scatter_about(keys[7], (EXPERTS, F, D), F ** -0.5, 0.15625, ((0, 8), (1, 4)))
    return dict(tokens=tokens, grad_out=grad_out, router_logits=router_logits, group_id=group_id, expert_ids=expert_ids, w_gate=w_gate, w_up=w_up, w_down=w_down)


def gate_weights(logits, group_ids, chosen, inside):
    probabilities = jax.nn.softmax(logits, axis=-1)
    columns = jnp.arange(logits.shape[1], dtype=jnp.int32)
    member = ((columns // GSIZE)[None, :] == group_ids[:, None]).astype(logits.dtype)
    group_mass = lax.optimization_barrier(jnp.sum(probabilities * member, axis=1))
    picked = lax.optimization_barrier(jnp.sum(jnp.where(chosen[:, :, None] == columns[None, None, :], logits[:, None, :], 0.0), axis=2))
    pair_share = jax.nn.softmax(picked, axis=-1)
    return jnp.where(inside[:, None], group_mass[:, None] * pair_share, 0.0)

def expert_pass(operands):
    rows_in, grads_in, gate_matrix, up_matrix, down_matrix = operands
    gate_pre = jnp.dot(rows_in, gate_matrix, preferred_element_type=jnp.float32)
    up_pre = jnp.dot(rows_in, up_matrix, preferred_element_type=jnp.float32)
    sigmoid_gate = jax.nn.sigmoid(gate_pre)
    activated = gate_pre * sigmoid_gate
    hidden = (activated * up_pre).astype(jnp.bfloat16)
    expert_out = jnp.dot(hidden, down_matrix, preferred_element_type=jnp.float32).astype(jnp.bfloat16)
    grad_hidden = jnp.dot(grads_in, down_matrix.T, preferred_element_type=jnp.float32)
    grad_gate_pre = (grad_hidden * up_pre * sigmoid_gate * (1.0 + gate_pre * (1.0 - sigmoid_gate))).astype(jnp.bfloat16)
    grad_up_pre = (grad_hidden * activated).astype(jnp.bfloat16)
    expert_back = (jnp.dot(grad_gate_pre, gate_matrix.T, preferred_element_type=jnp.float32) + jnp.dot(grad_up_pre, up_matrix.T, preferred_element_type=jnp.float32)).astype(jnp.bfloat16)
    gate_grad = jnp.dot(rows_in.T, grad_gate_pre, preferred_element_type=jnp.float32).astype(jnp.bfloat16)
    up_grad = jnp.dot(rows_in.T, grad_up_pre, preferred_element_type=jnp.float32).astype(jnp.bfloat16)
    down_grad = jnp.dot(hidden.T, grads_in, preferred_element_type=jnp.float32).astype(jnp.bfloat16)
    return (expert_out, expert_back, gate_grad, up_grad, down_grad)

def reference(tokens, grad_out, router_logits, group_id, expert_ids, w_gate, w_up, w_down):
    block_count = TOKENS // TOK_DEV
    inside = group_id < WGROUPS
    chosen = group_id[:, None] * GSIZE + expert_ids
    target = jnp.where(inside[:, None], chosen, EXPERTS)
    expert_range = jnp.arange(EXPERTS, dtype=jnp.int32)
    onehot = (target[:, :, None] == expert_range[None, None, :]).astype(jnp.int32)
    per_token = lax.optimization_barrier(jnp.sum(onehot, axis=1)).reshape(block_count, TOK_DEV, EXPERTS)
    earlier = (jnp.cumsum(per_token, axis=1) - per_token).reshape(TOKENS, 1, EXPERTS)
    slot_rank = lax.optimization_barrier(jnp.sum(onehot * earlier, axis=2))
    block_of = (jnp.arange(TOKENS, dtype=jnp.int32) // TOK_DEV)[:, None]
    slot_total = EXPERTS * block_count * CAP
    position = jnp.where(inside[:, None], (target * block_count + block_of) * CAP + slot_rank, slot_total).astype(jnp.int32)
    flat_position = position.reshape(-1)
    assignment_range = jnp.arange(2 * TOKENS, dtype=jnp.int32)
    assign_of = jnp.zeros((slot_total + 1,), jnp.int32).at[flat_position].set(assignment_range)
    filled = jnp.zeros((slot_total + 1,), jnp.int32).at[flat_position].set(1)
    filled = filled[:slot_total] > 0
    assign_used = assign_of[:slot_total]
    mix_weights, pull_back = jax.vjp(lambda values: gate_weights(values, group_id, chosen, inside), router_logits)
    grad_f32 = grad_out.astype(jnp.float32)
    weighted_grad = (mix_weights[:, :, None] * grad_f32[:, None, :]).astype(jnp.bfloat16).reshape(2 * TOKENS, D)
    token_rows = tokens[assign_used // 2]
    rows_buffer = jnp.where(filled[:, None], token_rows, jnp.zeros_like(token_rows)).reshape(EXPERTS, block_count * CAP, D)
    grad_rows = weighted_grad[assign_used]
    grads_buffer = jnp.where(filled[:, None], grad_rows, jnp.zeros_like(grad_rows)).reshape(EXPERTS, block_count * CAP, D)
    expert_out, expert_back, grad_gate, grad_up, grad_down = lax.map(expert_pass, (rows_buffer, grads_buffer, w_gate, w_up, w_down))
    out_flat = jnp.concatenate([expert_out.reshape(slot_total, D), jnp.zeros((1, D), expert_out.dtype)], axis=0)
    back_flat = jnp.concatenate([expert_back.reshape(slot_total, D), jnp.zeros((1, D), expert_back.dtype)], axis=0)
    out_rows = out_flat[position].astype(jnp.float32)
    back_rows = back_flat[position].astype(jnp.float32)
    mixed = lax.optimization_barrier(jnp.sum(mix_weights[:, :, None] * out_rows, axis=1)).astype(jnp.bfloat16)
    d_tokens = lax.optimization_barrier(jnp.sum(back_rows, axis=1)).astype(jnp.bfloat16)
    scores = lax.optimization_barrier(jnp.sum(grad_f32[:, None, :] * out_rows, axis=2))
    d_logits = pull_back(scores)[0]
    return (mixed, d_tokens, d_logits, grad_gate, grad_up, grad_down)
```

```python
import functools

import jax
import jax.numpy as jnp
from jax import lax
from jax.experimental import pallas as pl
from jax.experimental.pallas import tpu as pltpu
from jax.sharding import PartitionSpec as P

GSIZE = 8
CAP = 6
CHUNKS = 4
MESH = pl.DeviceIdType.MESH
F32 = jnp.float32
BF16 = jnp.bfloat16


def greet(n, z, node_count, local_count):
    barrier = pltpu.get_barrier_semaphore()
    for k in range(1, local_count):
        peer = lax.rem(z + k, local_count)
        pl.semaphore_signal(barrier, inc=1, device_id=(n, peer), device_id_type=MESH)
    for k in range(1, node_count):
        peer = lax.rem(n + k, node_count)
        pl.semaphore_signal(barrier, inc=1, device_id=(peer, z), device_id_type=MESH)
    pl.semaphore_wait(barrier, local_count + node_count - 2)


def split(value):
    high = value.astype(BF16)
    return high, (value - high.astype(F32)).astype(BF16)


def one_hots(meta, columns):
    lanes = lax.broadcasted_iota(jnp.int32, (meta.shape[0], columns), 1).astype(F32)
    return lanes == meta[:, 0:1], lanes == meta[:, 1:2]


def dispatch_kernel(
    node_count, local_count, rows, uniques,
    x_ref, meta_ref, out_ref, zmeta_ref,
    zbuf, sendbuf, high_ref, low_ref,
    zsend, zrecv, msend, mrecv, psend, precv, own_sem, place_sem,
):
    n, z = lax.axis_index("node"), lax.axis_index("local")
    width = x_ref.shape[1]
    step = width // CHUNKS
    own = pltpu.make_async_copy(x_ref, zbuf.at[z], own_sem.at[0])
    own.start()
    own_meta = pltpu.make_async_copy(meta_ref, zmeta_ref.at[z], own_sem.at[1])
    own_meta.start()
    greet(n, z, node_count, local_count)
    meta_copies, z_copies = [], []
    for k in range(1, local_count):
        peer = lax.rem(z + k, local_count)
        copy = pltpu.make_async_remote_copy(
            meta_ref, zmeta_ref.at[z], msend.at[k], mrecv.at[k],
            device_id=(n, peer), device_id_type=MESH)
        copy.start()
        meta_copies.append(copy)
    for c in range(CHUNKS):
        cols = pl.ds(c * step, step)
        for k in range(1, local_count):
            peer = lax.rem(z + k, local_count)
            copy = pltpu.make_async_remote_copy(
                x_ref.at[:, cols], zbuf.at[z, :, cols], zsend.at[c, k], zrecv.at[c, k],
                device_id=(n, peer), device_id_type=MESH)
            copy.start()
            z_copies.append(copy)
    own.wait()
    own_meta.wait()
    for copy in meta_copies:
        copy.wait()
    meta = zmeta_ref[...].reshape(local_count * 2 * uniques, 128)
    hot0, hot1 = one_hots(meta, node_count * 2 * rows)
    is_grad = meta[:, 4:5] > 0.5
    scale0 = jnp.where(is_grad, meta[:, 2:3], 1.0)
    scale1 = jnp.where(is_grad, meta[:, 3:4], 1.0)
    mix = jnp.where(hot0, scale0, 0.0) + jnp.where(hot1, scale1, 0.0)
    high, low = split(mix)
    high_ref[...] = high
    low_ref[...] = low
    p_copies, places = [], []
    for c in range(CHUNKS):
        cols = pl.ds(c * step, step)
        for k in range(1, local_count):
            z_copies[c * (local_count - 1) + k - 1].wait()
        block = zbuf[:, :, cols].reshape(local_count * 2 * uniques, step)
        contract = (((0,), (0,)), ((), ()))
        picked = lax.dot_general(
            high_ref[...], block, contract, preferred_element_type=F32
        ) + lax.dot_general(low_ref[...], block, contract, preferred_element_type=F32)
        sendbuf[:, :, cols] = picked.astype(BF16).reshape(node_count, 2 * rows, step)
        for k in range(1, node_count):
            peer = lax.rem(n + k, node_count)
            copy = pltpu.make_async_remote_copy(
                sendbuf.at[peer, :, cols], out_ref.at[n, :, cols],
                psend.at[c, k], precv.at[c, k],
                device_id=(peer, z), device_id_type=MESH)
            copy.start()
            p_copies.append(copy)
        place = pltpu.make_async_copy(
            sendbuf.at[n, :, cols], out_ref.at[n, :, cols], place_sem.at[c])
        place.start()
        places.append(place)
    for copy in places + p_copies:
        copy.wait()


def combine_kernel(
    node_count, local_count, rows, uniques,
    part_ref, q_ref, zmeta_ref, out_ref, qout_ref,
    pbuf, qbuf, sendbuf, qsend, rbuf, rqbuf, high_ref, low_ref,
    psend, precv, qpsend, qprecv, zsend, zrecv, qzsend, qzrecv, own_sem,
):
    n, z = lax.axis_index("node"), lax.axis_index("local")
    width = part_ref.shape[2]
    step = width // CHUNKS
    own = pltpu.make_async_copy(part_ref.at[n], pbuf.at[n], own_sem.at[0])
    own.start()
    own_q = pltpu.make_async_copy(q_ref.at[n], qbuf.at[n], own_sem.at[1])
    own_q.start()
    greet(n, z, node_count, local_count)
    p_copies, q_copies = [], []
    for k in range(1, node_count):
        peer = lax.rem(n + k, node_count)
        copy = pltpu.make_async_remote_copy(
            q_ref.at[peer], qbuf.at[n], qpsend.at[k], qprecv.at[k],
            device_id=(peer, z), device_id_type=MESH)
        copy.start()
        q_copies.append(copy)
    for c in range(CHUNKS):
        cols = pl.ds(c * step, step)
        for k in range(1, node_count):
            peer = lax.rem(n + k, node_count)
            copy = pltpu.make_async_remote_copy(
                part_ref.at[peer, :, cols], pbuf.at[n, :, cols],
                psend.at[c, k], precv.at[c, k],
                device_id=(peer, z), device_id_type=MESH)
            copy.start()
            p_copies.append(copy)
    meta = zmeta_ref[...].reshape(local_count * 2 * uniques, 128)
    hot0, hot1 = one_hots(meta, node_count * 2 * rows)
    is_grad = meta[:, 4:5] > 0.5
    scale0 = jnp.where(is_grad, 1.0, meta[:, 2:3])
    scale1 = jnp.where(is_grad, 1.0, meta[:, 3:4])
    mix = jnp.where(hot0, scale0, 0.0) + jnp.where(hot1, scale1, 0.0)
    high, low = split(mix)
    high_ref[...] = high
    low_ref[...] = low
    own.wait()
    own_q.wait()
    for copy in q_copies:
        copy.wait()
    q_all = qbuf[...].reshape(node_count * 2 * rows, 128)
    q0 = jnp.dot(jnp.where(hot0, 1.0, 0.0), q_all, preferred_element_type=F32,
                 precision=lax.Precision.HIGHEST)
    q1 = jnp.dot(jnp.where(hot1, 1.0, 0.0), q_all, preferred_element_type=F32,
                 precision=lax.Precision.HIGHEST)
    lane = lax.broadcasted_iota(jnp.int32, q0.shape, 1)
    qsend[...] = jnp.where(lane == 0, q0, q1).reshape(local_count, 2 * uniques, 128)
    z_copies, qz_copies = [], []
    for c in range(CHUNKS):
        cols = pl.ds(c * step, step)
        for k in range(1, node_count):
            p_copies[c * (node_count - 1) + k - 1].wait()
        block = pbuf[:, :, cols].reshape(node_count * 2 * rows, step)
        summed = jnp.dot(high_ref[...], block, preferred_element_type=F32) + jnp.dot(
            low_ref[...], block, preferred_element_type=F32)
        sendbuf[:, :, cols] = summed.astype(BF16).reshape(local_count, 2 * uniques, step)
        for k in range(1, local_count):
            peer = lax.rem(z + k, local_count)
            copy = pltpu.make_async_remote_copy(
                sendbuf.at[peer, :, cols], rbuf.at[k, :, cols],
                zsend.at[c, k], zrecv.at[c, k],
                device_id=(n, peer), device_id_type=MESH)
            copy.start()
            z_copies.append(copy)
            if c == 0:
                copy = pltpu.make_async_remote_copy(
                    qsend.at[peer], rqbuf.at[k], qzsend.at[k], qzrecv.at[k],
                    device_id=(n, peer), device_id_type=MESH)
                copy.start()
                qz_copies.append(copy)
    for copy in qz_copies:
        copy.wait()
    q_total = qsend[z]
    for k in range(1, local_count):
        q_total = q_total + rqbuf[k]
    qout_ref[...] = q_total
    for c in range(CHUNKS):
        cols = pl.ds(c * step, step)
        for k in range(1, local_count):
            z_copies[c * (local_count - 1) + k - 1].wait()
        total = sendbuf[z, :, cols].astype(F32)
        for k in range(1, local_count):
            total = total + rbuf[k, :, cols].astype(F32)
        out_ref[:, cols] = total.astype(BF16)


def vmem(count):
    return [pl.BlockSpec(memory_space=pltpu.VMEM)] * count


def dispatch(x, meta, node_count, local_count, rows, uniques):
    width = x.shape[1]
    dma = pltpu.SemaphoreType.DMA
    shape = (local_count * 2 * uniques, node_count * 2 * rows)
    return pl.pallas_call(
        functools.partial(dispatch_kernel, node_count, local_count, rows, uniques),
        out_shape=(
            jax.ShapeDtypeStruct((node_count, 2 * rows, width), BF16),
            jax.ShapeDtypeStruct((local_count, 2 * uniques, 128), F32),
        ),
        in_specs=vmem(2),
        out_specs=tuple(vmem(2)),
        scratch_shapes=[
            pltpu.VMEM((local_count, 2 * uniques, width), BF16),
            pltpu.VMEM((node_count, 2 * rows, width), BF16),
            pltpu.VMEM(shape, BF16),
            pltpu.VMEM(shape, BF16),
            dma((CHUNKS, local_count)), dma((CHUNKS, local_count)),
            dma((local_count,)), dma((local_count,)),
            dma((CHUNKS, node_count)), dma((CHUNKS, node_count)),
            dma((2,)), dma((CHUNKS,)),
        ],
        compiler_params=pltpu.CompilerParams(
            collective_id=0, has_side_effects=True, vmem_limit_bytes=60 * 2**20),
    )(x, meta)


def combine(parts, q_rows, zmeta, node_count, local_count, rows, uniques):
    width = parts.shape[2]
    dma = pltpu.SemaphoreType.DMA
    shape = (local_count * 2 * uniques, node_count * 2 * rows)
    return pl.pallas_call(
        functools.partial(combine_kernel, node_count, local_count, rows, uniques),
        out_shape=(
            jax.ShapeDtypeStruct((2 * uniques, width), BF16),
            jax.ShapeDtypeStruct((2 * uniques, 128), F32),
        ),
        in_specs=vmem(3),
        out_specs=tuple(vmem(2)),
        scratch_shapes=[
            pltpu.VMEM((node_count, 2 * rows, width), BF16),
            pltpu.VMEM((node_count, 2 * rows, 128), F32),
            pltpu.VMEM((local_count, 2 * uniques, width), BF16),
            pltpu.VMEM((local_count, 2 * uniques, 128), F32),
            pltpu.VMEM((local_count, 2 * uniques, width), BF16),
            pltpu.VMEM((local_count, 2 * uniques, 128), F32),
            pltpu.VMEM(shape, BF16),
            pltpu.VMEM(shape, BF16),
            dma((CHUNKS, node_count)), dma((CHUNKS, node_count)),
            dma((node_count,)), dma((node_count,)),
            dma((CHUNKS, local_count)), dma((CHUNKS, local_count)),
            dma((local_count,)), dma((local_count,)),
            dma((2,)),
        ],
        compiler_params=pltpu.CompilerParams(
            collective_id=1, has_side_effects=True, vmem_limit_bytes=60 * 2**20),
    )(parts, q_rows, zmeta)


def body(tokens, grad_out, router_logits, group_id, expert_ids, w_gate, w_up, w_down):
    owned = w_gate.shape[0]
    node_count = lax.axis_size("node")
    local_count = lax.axis_size("local")
    z = lax.axis_index("local")
    token_count, width = tokens.shape
    expert_total = owned * node_count
    window_groups = expert_total // GSIZE
    slots = owned * CAP
    rows = local_count * slots
    uniques = min(token_count, node_count * slots // 2)

    inside = group_id < window_groups
    chosen = group_id[:, None] * GSIZE + expert_ids
    target = jnp.where(inside[:, None], chosen, expert_total)
    expert_range = jnp.arange(expert_total, dtype=jnp.int32)
    onehot = target[:, :, None] == expert_range[None, None, :]
    per_token = jnp.sum(onehot.astype(F32), axis=1)
    counted = jnp.concatenate([per_token, inside[:, None].astype(F32)], axis=1).astype(BF16)
    order = jnp.arange(token_count, dtype=jnp.int32)
    before = (order[None, :] < order[:, None]).astype(BF16)
    earlier = jnp.dot(before, counted, preferred_element_type=F32)
    slot_rank = jnp.sum(jnp.where(onehot, earlier[:, None, :-1], 0.0), axis=2).astype(jnp.int32)
    unique_rank = earlier[:, -1].astype(jnp.int32)
    picks = (
        (jnp.arange(uniques, dtype=jnp.int32)[:, None] == unique_rank[None, :]) & inside[None, :]
    )
    dest = (target // owned) * (2 * rows) + z * slots + (target % owned) * CAP + slot_rank

    probabilities = jax.nn.softmax(router_logits, axis=-1)
    columns = jnp.arange(router_logits.shape[1], dtype=jnp.int32)
    member = (columns // GSIZE)[None, :] == group_id[:, None]
    mass = jnp.sum(jnp.where(member, probabilities, 0.0), axis=1)
    here = chosen[:, :, None] == columns[None, None, :]
    picked = jnp.sum(jnp.where(here, router_logits[:, None, :], 0.0), axis=2)
    share = jax.nn.softmax(picked, axis=-1)
    weights = jnp.where(inside[:, None], mass[:, None] * share, 0.0)

    pick_bf16 = picks.astype(BF16)
    x = jnp.concatenate(
        [jnp.dot(pick_bf16, tokens, preferred_element_type=F32).astype(BF16),
         jnp.dot(pick_bf16, grad_out, preferred_element_type=F32).astype(BF16)], axis=0)
    facts = jnp.concatenate([dest.astype(F32) + 1.0, weights], axis=1)
    facts = jnp.sum(jnp.where(picks[:, :, None], facts[None], 0.0), axis=1)
    base = facts[:, :2] - 1.0
    moved = jnp.where(base < 0.0, -1.0, base + rows)
    zeros = jnp.zeros((uniques, 1), F32)
    meta = jnp.concatenate(
        [jnp.concatenate([base, facts[:, 2:], zeros], axis=1),
         jnp.concatenate([moved, facts[:, 2:], zeros + 1.0], axis=1)], axis=0)
    meta = jnp.pad(meta, ((0, 0), (0, 123)))

    arrived, zmeta = dispatch(x, meta, node_count, local_count, rows, uniques)

    def by_expert(part):
        part = part.reshape(node_count, local_count, owned, CAP, width)
        return part.transpose(2, 0, 1, 3, 4).reshape(owned, node_count * local_count * CAP, width)

    def by_node(part):
        last = part.shape[-1]
        part = part.reshape(owned, node_count, local_count, CAP, last)
        return part.transpose(1, 2, 0, 3, 4).reshape(node_count, rows, last)

    rows_in = by_expert(arrived[:, :rows])
    grads_in = by_expert(arrived[:, rows:])
    gate_pre = jnp.einsum("erd,edf->erf", rows_in, w_gate, preferred_element_type=F32)
    up_pre = jnp.einsum("erd,edf->erf", rows_in, w_up, preferred_element_type=F32)
    sigmoid_gate = jax.nn.sigmoid(gate_pre)
    activated = gate_pre * sigmoid_gate
    hidden = (activated * up_pre).astype(BF16)
    grad_hidden = jnp.einsum("erd,efd->erf", grads_in, w_down, preferred_element_type=F32)
    grad_gate_pre = (
        grad_hidden * up_pre * sigmoid_gate * (1.0 + gate_pre * (1.0 - sigmoid_gate))
    ).astype(BF16)
    grad_up_pre = (grad_hidden * activated).astype(BF16)
    q_part = jnp.sum(hidden.astype(F32) * grad_hidden, axis=2, keepdims=True)
    partial_out = jnp.einsum("erf,efd->erd", hidden, w_down, preferred_element_type=F32)
    partial_in = jnp.einsum(
        "erf,edf->erd", grad_gate_pre, w_gate, preferred_element_type=F32
    ) + jnp.einsum("erf,edf->erd", grad_up_pre, w_up, preferred_element_type=F32)
    parts = jnp.concatenate(
        [by_node(partial_out.astype(BF16)), by_node(partial_in.astype(BF16))], axis=1)
    q_rows = by_node(jnp.broadcast_to(q_part, q_part.shape[:2] + (128,)))
    q_rows = jnp.concatenate([q_rows, q_rows], axis=1)
    grad_gate = jnp.einsum(
        "erd,erf->edf", rows_in, grad_gate_pre, preferred_element_type=F32).astype(BF16)
    grad_up = jnp.einsum(
        "erd,erf->edf", rows_in, grad_up_pre, preferred_element_type=F32).astype(BF16)
    grad_down = jnp.einsum(
        "erf,erd->efd", hidden, grads_in, preferred_element_type=F32).astype(BF16)

    results, q_unique = combine(parts, q_rows, zmeta, node_count, local_count, rows, uniques)

    mixed = jnp.einsum("ut,ud->td", pick_bf16, results[:uniques],
                       preferred_element_type=F32).astype(BF16)
    d_tokens = jnp.einsum("ut,ud->td", pick_bf16, results[uniques:],
                          preferred_element_type=F32).astype(BF16)
    q = jnp.sum(jnp.where(picks[:, :, None], q_unique[:uniques, None, :2], 0.0), axis=0)
    q_sum = q[:, 0:1] + q[:, 1:2]
    lean = share[:, 1:2] * q[:, 0:1] - share[:, 0:1] * q[:, 1:2]
    inner = jnp.where(member, router_logits, -jnp.inf)
    inner = jax.nn.softmax(inner, axis=-1)
    tilt = here[:, 0].astype(F32) - here[:, 1].astype(F32)
    d_logits = q_sum * (inner - probabilities) + lean * tilt
    return (mixed, d_tokens, d_logits, grad_gate, grad_up, grad_down)


def solution(mesh):
    rows = P(("node", "local"), None)
    return jax.shard_map(
        body,
        mesh=mesh,
        in_specs=(
            rows, rows, rows, P(("node", "local")), rows,
            P("node", None, "local"), P("node", None, "local"), P("node", "local", None),
        ),
        out_specs=(
            rows, rows, rows,
            P("node", None, "local"), P("node", None, "local"), P("node", "local", None),
        ),
        check_vma=False,
    )
```

```python
import functools

import jax
import jax.numpy as jnp
from jax import lax
from jax.experimental import pallas as pl
from jax.experimental.pallas import tpu as pltpu
from jax.sharding import PartitionSpec as P

GSIZE = 8
CAP = 6
CHUNKS = 4
FUSED_CHUNKS = 8
MESH = pl.DeviceIdType.MESH
F32 = jnp.float32
BF16 = jnp.bfloat16


def greet(n, z, node_count, local_count):
    barrier = pltpu.get_barrier_semaphore()
    for k in range(1, local_count):
        peer = lax.rem(z + k, local_count)
        pl.semaphore_signal(barrier, inc=1, device_id=(n, peer), device_id_type=MESH)
    for k in range(1, node_count):
        peer = lax.rem(n + k, node_count)
        pl.semaphore_signal(barrier, inc=1, device_id=(peer, z), device_id_type=MESH)
    pl.semaphore_wait(barrier, local_count + node_count - 2)


def split(value):
    high = value.astype(BF16)
    return high, (value - high.astype(F32)).astype(BF16)


def one_hots(meta, columns):
    lanes = lax.broadcasted_iota(jnp.int32, (meta.shape[0], columns), 1).astype(F32)
    return lanes == meta[:, 0:1], lanes == meta[:, 1:2]


def dispatch_kernel(
    node_count, local_count, rows, uniques,
    x_ref, meta_ref, out_ref, zmeta_ref,
    zbuf, sendbuf, high_ref, low_ref,
    zsend, zrecv, msend, mrecv, psend, precv, own_sem, place_sem,
):
    n, z = lax.axis_index("node"), lax.axis_index("local")
    width = x_ref.shape[1]
    step = width // CHUNKS
    own = pltpu.make_async_copy(x_ref, zbuf.at[z], own_sem.at[0])
    own.start()
    own_meta = pltpu.make_async_copy(meta_ref, zmeta_ref.at[z], own_sem.at[1])
    own_meta.start()
    greet(n, z, node_count, local_count)
    meta_copies, z_copies = [], []
    for k in range(1, local_count):
        peer = lax.rem(z + k, local_count)
        copy = pltpu.make_async_remote_copy(
            meta_ref, zmeta_ref.at[z], msend.at[k], mrecv.at[k],
            device_id=(n, peer), device_id_type=MESH)
        copy.start()
        meta_copies.append(copy)
    for c in range(CHUNKS):
        cols = pl.ds(c * step, step)
        for k in range(1, local_count):
            peer = lax.rem(z + k, local_count)
            copy = pltpu.make_async_remote_copy(
                x_ref.at[:, cols], zbuf.at[z, :, cols], zsend.at[c, k], zrecv.at[c, k],
                device_id=(n, peer), device_id_type=MESH)
            copy.start()
            z_copies.append(copy)
    own.wait()
    own_meta.wait()
    for copy in meta_copies:
        copy.wait()
    meta = zmeta_ref[...].reshape(local_count * 2 * uniques, 128)
    hot0, hot1 = one_hots(meta, node_count * 2 * rows)
    is_grad = meta[:, 4:5] > 0.5
    scale0 = jnp.where(is_grad, meta[:, 2:3], 1.0)
    scale1 = jnp.where(is_grad, meta[:, 3:4], 1.0)
    mix = jnp.where(hot0, scale0, 0.0) + jnp.where(hot1, scale1, 0.0)
    high, low = split(mix)
    high_ref[...] = high
    low_ref[...] = low
    p_copies, places = [], []
    for c in range(CHUNKS):
        cols = pl.ds(c * step, step)
        for k in range(1, local_count):
            z_copies[c * (local_count - 1) + k - 1].wait()
        block = zbuf[:, :, cols].reshape(local_count * 2 * uniques, step)
        contract = (((0,), (0,)), ((), ()))
        picked = lax.dot_general(
            high_ref[...], block, contract, preferred_element_type=F32
        ) + lax.dot_general(low_ref[...], block, contract, preferred_element_type=F32)
        sendbuf[:, :, cols] = picked.astype(BF16).reshape(node_count, 2 * rows, step)
        for k in range(1, node_count):
            peer = lax.rem(n + k, node_count)
            copy = pltpu.make_async_remote_copy(
                sendbuf.at[peer, :, cols], out_ref.at[n, :, cols],
                psend.at[c, k], precv.at[c, k],
                device_id=(peer, z), device_id_type=MESH)
            copy.start()
            p_copies.append(copy)
        place = pltpu.make_async_copy(
            sendbuf.at[n, :, cols], out_ref.at[n, :, cols], place_sem.at[c])
        place.start()
        places.append(place)
    for copy in places + p_copies:
        copy.wait()


def combine_kernel(
    node_count, local_count, rows, uniques,
    part_ref, q_ref, zmeta_ref, out_ref, qout_ref,
    pbuf, qbuf, sendbuf, qsend, rbuf, rqbuf, high_ref, low_ref,
    psend, precv, qpsend, qprecv, zsend, zrecv, qzsend, qzrecv, own_sem,
):
    n, z = lax.axis_index("node"), lax.axis_index("local")
    width = part_ref.shape[2]
    step = width // CHUNKS
    own = pltpu.make_async_copy(part_ref.at[n], pbuf.at[n], own_sem.at[0])
    own.start()
    own_q = pltpu.make_async_copy(q_ref.at[n], qbuf.at[n], own_sem.at[1])
    own_q.start()
    greet(n, z, node_count, local_count)
    p_copies, q_copies = [], []
    for k in range(1, node_count):
        peer = lax.rem(n + k, node_count)
        copy = pltpu.make_async_remote_copy(
            q_ref.at[peer], qbuf.at[n], qpsend.at[k], qprecv.at[k],
            device_id=(peer, z), device_id_type=MESH)
        copy.start()
        q_copies.append(copy)
    for c in range(CHUNKS):
        cols = pl.ds(c * step, step)
        for k in range(1, node_count):
            peer = lax.rem(n + k, node_count)
            copy = pltpu.make_async_remote_copy(
                part_ref.at[peer, :, cols], pbuf.at[n, :, cols],
                psend.at[c, k], precv.at[c, k],
                device_id=(peer, z), device_id_type=MESH)
            copy.start()
            p_copies.append(copy)
    meta = zmeta_ref[...].reshape(local_count * 2 * uniques, 128)
    hot0, hot1 = one_hots(meta, node_count * 2 * rows)
    is_grad = meta[:, 4:5] > 0.5
    scale0 = jnp.where(is_grad, 1.0, meta[:, 2:3])
    scale1 = jnp.where(is_grad, 1.0, meta[:, 3:4])
    mix = jnp.where(hot0, scale0, 0.0) + jnp.where(hot1, scale1, 0.0)
    high, low = split(mix)
    high_ref[...] = high
    low_ref[...] = low
    own.wait()
    own_q.wait()
    for copy in q_copies:
        copy.wait()
    q_all = qbuf[...].reshape(node_count * 2 * rows, 128)
    q0 = jnp.dot(jnp.where(hot0, 1.0, 0.0), q_all, preferred_element_type=F32,
                 precision=lax.Precision.HIGHEST)
    q1 = jnp.dot(jnp.where(hot1, 1.0, 0.0), q_all, preferred_element_type=F32,
                 precision=lax.Precision.HIGHEST)
    lane = lax.broadcasted_iota(jnp.int32, q0.shape, 1)
    qsend[...] = jnp.where(lane == 0, q0, q1).reshape(local_count, 2 * uniques, 128)
    z_copies, qz_copies = [], []
    for c in range(CHUNKS):
        cols = pl.ds(c * step, step)
        for k in range(1, node_count):
            p_copies[c * (node_count - 1) + k - 1].wait()
        block = pbuf[:, :, cols].reshape(node_count * 2 * rows, step)
        summed = jnp.dot(high_ref[...], block, preferred_element_type=F32) + jnp.dot(
            low_ref[...], block, preferred_element_type=F32)
        sendbuf[:, :, cols] = summed.astype(BF16).reshape(local_count, 2 * uniques, step)
        for k in range(1, local_count):
            peer = lax.rem(z + k, local_count)
            copy = pltpu.make_async_remote_copy(
                sendbuf.at[peer, :, cols], rbuf.at[k, :, cols],
                zsend.at[c, k], zrecv.at[c, k],
                device_id=(n, peer), device_id_type=MESH)
            copy.start()
            z_copies.append(copy)
            if c == 0:
                copy = pltpu.make_async_remote_copy(
                    qsend.at[peer], rqbuf.at[k], qzsend.at[k], qzrecv.at[k],
                    device_id=(n, peer), device_id_type=MESH)
                copy.start()
                qz_copies.append(copy)
    for copy in qz_copies:
        copy.wait()
    q_total = qsend[z]
    for k in range(1, local_count):
        q_total = q_total + rqbuf[k]
    qout_ref[...] = q_total
    for c in range(CHUNKS):
        cols = pl.ds(c * step, step)
        for k in range(1, local_count):
            z_copies[c * (local_count - 1) + k - 1].wait()
        total = sendbuf[z, :, cols].astype(F32)
        for k in range(1, local_count):
            total = total + rbuf[k, :, cols].astype(F32)
        out_ref[:, cols] = total.astype(BF16)


def vmem(count):
    return [pl.BlockSpec(memory_space=pltpu.VMEM)] * count


def dispatch(x, meta, node_count, local_count, rows, uniques):
    width = x.shape[1]
    dma = pltpu.SemaphoreType.DMA
    shape = (local_count * 2 * uniques, node_count * 2 * rows)
    return pl.pallas_call(
        functools.partial(dispatch_kernel, node_count, local_count, rows, uniques),
        out_shape=(
            jax.ShapeDtypeStruct((node_count, 2 * rows, width), BF16),
            jax.ShapeDtypeStruct((local_count, 2 * uniques, 128), F32),
        ),
        in_specs=vmem(2),
        out_specs=tuple(vmem(2)),
        scratch_shapes=[
            pltpu.VMEM((local_count, 2 * uniques, width), BF16),
            pltpu.VMEM((node_count, 2 * rows, width), BF16),
            pltpu.VMEM(shape, BF16),
            pltpu.VMEM(shape, BF16),
            dma((CHUNKS, local_count)), dma((CHUNKS, local_count)),
            dma((local_count,)), dma((local_count,)),
            dma((CHUNKS, node_count)), dma((CHUNKS, node_count)),
            dma((2,)), dma((CHUNKS,)),
        ],
        compiler_params=pltpu.CompilerParams(
            collective_id=0, has_side_effects=True, vmem_limit_bytes=60 * 2**20),
    )(x, meta)


def combine(parts, q_rows, zmeta, node_count, local_count, rows, uniques):
    width = parts.shape[2]
    dma = pltpu.SemaphoreType.DMA
    shape = (local_count * 2 * uniques, node_count * 2 * rows)
    return pl.pallas_call(
        functools.partial(combine_kernel, node_count, local_count, rows, uniques),
        out_shape=(
            jax.ShapeDtypeStruct((2 * uniques, width), BF16),
            jax.ShapeDtypeStruct((2 * uniques, 128), F32),
        ),
        in_specs=vmem(3),
        out_specs=tuple(vmem(2)),
        scratch_shapes=[
            pltpu.VMEM((node_count, 2 * rows, width), BF16),
            pltpu.VMEM((node_count, 2 * rows, 128), F32),
            pltpu.VMEM((local_count, 2 * uniques, width), BF16),
            pltpu.VMEM((local_count, 2 * uniques, 128), F32),
            pltpu.VMEM((local_count, 2 * uniques, width), BF16),
            pltpu.VMEM((local_count, 2 * uniques, 128), F32),
            pltpu.VMEM(shape, BF16),
            pltpu.VMEM(shape, BF16),
            dma((CHUNKS, node_count)), dma((CHUNKS, node_count)),
            dma((node_count,)), dma((node_count,)),
            dma((CHUNKS, local_count)), dma((CHUNKS, local_count)),
            dma((local_count,)), dma((local_count,)),
            dma((2,)),
        ],
        compiler_params=pltpu.CompilerParams(
            collective_id=1, has_side_effects=True, vmem_limit_bytes=60 * 2**20),
    )(parts, q_rows, zmeta)


def layer_kernel(
    node_count, local_count, rows, uniques, chunks,
    x_ref, meta_ref, gate_hbm, up_hbm, down_hbm,
    arrived_ref, hidden_ref, dgate_ref, dup_ref, out_ref, qout_ref,
    zmeta, zbuf, sendbuf, high_ref, low_ref, back_high, back_low,
    gate_ref, up_ref, down_ref, gate_acc, up_acc, down_acc,
    parts, pbuf, q_rows, qbuf, sums, qsums, rbuf, rqbuf,
    zsend, zrecv, msend, mrecv, psend, precv, psend2, precv2, zsend2, zrecv2,
    qsend, qrecv, qsend2, qrecv2, own_sem, place_sem, weight_sem,
):
    n, z = lax.axis_index("node"), lax.axis_index("local")
    width = x_ref.shape[1]
    step = width // chunks
    total_rows = node_count * 2 * rows
    total_uniques = local_count * 2 * uniques

    def cols(c):
        return pl.ds(pl.multiple_of(c * step, step), step)

    def remote(src, dst, send, recv, device):
        return pltpu.make_async_remote_copy(
            src, dst, send, recv, device_id=device, device_id_type=MESH)

    def z_peer(k):
        return lax.rem(z + k, local_count)

    def n_peer(k):
        return lax.rem(n + k, node_count)

    def z_copy(c, k):
        return remote(x_ref.at[:, cols(c)], zbuf.at[z, :, cols(c)],
                      zsend.at[c, k], zrecv.at[c, k], (n, z_peer(k)))

    def p_copy(c, k):
        return remote(sendbuf.at[n_peer(k), :, cols(c)], arrived_ref.at[n, :, cols(c)],
                      psend.at[c, k], precv.at[c, k], (n_peer(k), z))

    def place(c):
        return pltpu.make_async_copy(
            sendbuf.at[n, :, cols(c)], arrived_ref.at[n, :, cols(c)], place_sem.at[c])

    def p_copy2(c, k):
        return remote(parts.at[n_peer(k), :, cols(c)], pbuf.at[n, :, cols(c)],
                      psend2.at[c, k], precv2.at[c, k], (n_peer(k), z))

    def place2(c):
        return pltpu.make_async_copy(
            parts.at[n, :, cols(c)], pbuf.at[n, :, cols(c)], place_sem.at[chunks + c])

    def z_copy2(c, k):
        return remote(sums.at[z_peer(k), :, cols(c)], rbuf.at[k, :, cols(c)],
                      zsend2.at[c, k], zrecv2.at[c, k], (n, z_peer(k)))

    weights = [
        pltpu.make_async_copy(gate_hbm, gate_ref, weight_sem.at[0]),
        pltpu.make_async_copy(up_hbm, up_ref, weight_sem.at[1]),
        pltpu.make_async_copy(down_hbm, down_ref, weight_sem.at[2]),
    ]
    own = pltpu.make_async_copy(x_ref, zbuf.at[z], own_sem.at[0])
    own.start()
    own_meta = pltpu.make_async_copy(meta_ref, zmeta.at[z], own_sem.at[1])
    own_meta.start()
    greet(n, z, node_count, local_count)
    meta_copies = [
        remote(meta_ref, zmeta.at[z], msend.at[k], mrecv.at[k], (n, z_peer(k)))
        for k in range(1, local_count)
    ]
    for copy in meta_copies:
        copy.start()

    @pl.loop(0, chunks)
    def _(c):
        for k in range(1, local_count):
            z_copy(c, k).start()

    for copy in weights:
        copy.start()
    gate_acc[...] = jnp.zeros_like(gate_acc)
    up_acc[...] = jnp.zeros_like(up_acc)
    down_acc[...] = jnp.zeros_like(down_acc)
    own.wait()
    own_meta.wait()
    for copy in meta_copies:
        copy.wait()
    meta = zmeta[...].reshape(total_uniques, 128)
    hot0, hot1 = one_hots(meta, total_rows)
    is_grad = meta[:, 4:5] > 0.5
    w0, w1 = meta[:, 2:3], meta[:, 3:4]
    mix = jnp.where(hot0, jnp.where(is_grad, w0, 1.0), 0.0) + jnp.where(
        hot1, jnp.where(is_grad, w1, 1.0), 0.0)
    high_ref[...], low_ref[...] = split(mix)
    mix = jnp.where(hot0, jnp.where(is_grad, 1.0, w0), 0.0) + jnp.where(
        hot1, jnp.where(is_grad, 1.0, w1), 0.0)
    back_high[...], back_low[...] = split(mix)
    over_rows = (((0,), (0,)), ((), ()))
    over_last = (((1,), (1,)), ((), ()))

    def gather(c):
        for k in range(1, node_count):
            p_copy(c, k).wait()
        place(c).wait()
        block = arrived_ref[:, :, cols(c)].reshape(total_rows, step)
        gate_acc[...] += jnp.dot(block, gate_ref[cols(c), :], preferred_element_type=F32)
        up_acc[...] += jnp.dot(block, up_ref[cols(c), :], preferred_element_type=F32)
        down_acc[...] += lax.dot_general(
            block, down_ref[:, cols(c)], over_last, preferred_element_type=F32)

    @pl.loop(0, chunks)
    def _(c):
        for k in range(1, local_count):
            z_copy(c, k).wait()
        block = zbuf[:, :, cols(c)].reshape(total_uniques, step)
        picked = lax.dot_general(
            high_ref[...], block, over_rows, preferred_element_type=F32
        ) + lax.dot_general(low_ref[...], block, over_rows, preferred_element_type=F32)
        sendbuf[:, :, cols(c)] = picked.astype(BF16).reshape(node_count, 2 * rows, step)
        for k in range(1, node_count):
            p_copy(c, k).start()
        place(c).start()

        @pl.when(c == 0)
        def _():
            for copy in weights:
                copy.wait()

        @pl.when(c > 0)
        def _():
            gather(c - 1)

    gather(chunks - 1)

    hidden_units = gate_acc.shape[1]

    def half(acc, kind):
        whole = acc[...].reshape(node_count, 2 * rows, hidden_units)
        return whole[:, kind * rows:(kind + 1) * rows].reshape(node_count * rows, hidden_units)

    gate_pre, up_pre, grad_hidden = half(gate_acc, 0), half(up_acc, 0), half(down_acc, 1)
    sigmoid_gate = jax.nn.sigmoid(gate_pre)
    activated = gate_pre * sigmoid_gate
    hidden = (activated * up_pre).astype(BF16)
    hidden_ref[...] = hidden
    dgate_ref[...] = (
        grad_hidden * up_pre * sigmoid_gate * (1.0 + gate_pre * (1.0 - sigmoid_gate))
    ).astype(BF16)
    dup_ref[...] = (grad_hidden * activated).astype(BF16)
    q_part = jnp.sum(hidden.astype(F32) * grad_hidden, axis=1, keepdims=True)
    q_part = jnp.broadcast_to(q_part, (node_count * rows, 128)).reshape(node_count, rows, 128)
    q_rows[...] = jnp.concatenate([q_part, q_part], axis=1)

    def return_sums(c):
        for k in range(1, node_count):
            p_copy2(c, k).wait()
        place2(c).wait()
        block = pbuf[:, :, cols(c)].reshape(total_rows, step)
        summed = jnp.dot(back_high[...], block, preferred_element_type=F32) + jnp.dot(
            back_low[...], block, preferred_element_type=F32)
        sums[:, :, cols(c)] = summed.astype(BF16).reshape(local_count, 2 * uniques, step)
        for k in range(1, local_count):
            z_copy2(c, k).start()

    @pl.loop(0, chunks)
    def _(c):
        part_out = jnp.dot(hidden_ref[...], down_ref[:, cols(c)], preferred_element_type=F32)
        part_in = lax.dot_general(
            dgate_ref[...], gate_ref[cols(c), :], over_last, preferred_element_type=F32
        ) + lax.dot_general(
            dup_ref[...], up_ref[cols(c), :], over_last, preferred_element_type=F32)
        both = jnp.concatenate(
            [part_out.reshape(node_count, rows, step), part_in.reshape(node_count, rows, step)],
            axis=1)
        parts[:, :, cols(c)] = both.astype(BF16)
        for k in range(1, node_count):
            p_copy2(c, k).start()
        place2(c).start()

        @pl.when(c > 0)
        def _():
            return_sums(c - 1)

    q_own = pltpu.make_async_copy(q_rows.at[n], qbuf.at[n], own_sem.at[2])
    q_own.start()
    q_copies = [
        remote(q_rows.at[n_peer(k)], qbuf.at[n], qsend.at[k], qrecv.at[k], (n_peer(k), z))
        for k in range(1, node_count)
    ]
    for copy in q_copies:
        copy.start()
    return_sums(chunks - 1)
    q_own.wait()
    for copy in q_copies:
        copy.wait()
    meta = zmeta[...].reshape(total_uniques, 128)
    hot0, hot1 = one_hots(meta, total_rows)
    q_all = qbuf[...].reshape(total_rows, 128)
    q0 = jnp.dot(jnp.where(hot0, 1.0, 0.0), q_all, preferred_element_type=F32,
                 precision=lax.Precision.HIGHEST)
    q1 = jnp.dot(jnp.where(hot1, 1.0, 0.0), q_all, preferred_element_type=F32,
                 precision=lax.Precision.HIGHEST)
    lane = lax.broadcasted_iota(jnp.int32, q0.shape, 1)
    qsums[...] = jnp.where(lane == 0, q0, q1).reshape(local_count, 2 * uniques, 128)
    q_copies = [
        remote(qsums.at[z_peer(k)], rqbuf.at[k], qsend2.at[k], qrecv2.at[k], (n, z_peer(k)))
        for k in range(1, local_count)
    ]
    for copy in q_copies:
        copy.start()

    @pl.loop(0, chunks)
    def _(c):
        for k in range(1, local_count):
            z_copy2(c, k).wait()
        total = sums[z, :, cols(c)].astype(F32)
        for k in range(1, local_count):
            total = total + rbuf[k, :, cols(c)].astype(F32)
        out_ref[:, cols(c)] = total.astype(BF16)

    for copy in q_copies:
        copy.wait()
    q_total = qsums[z]
    for k in range(1, local_count):
        q_total = q_total + rqbuf[k]
    qout_ref[...] = q_total


def layer(x, meta, gate, up, down, node_count, local_count, rows, uniques, chunks):
    width, units = gate.shape
    dma = pltpu.SemaphoreType.DMA
    shape = (local_count * 2 * uniques, node_count * 2 * rows)
    by_node = pltpu.VMEM((node_count, 2 * rows, width), BF16)
    by_node_q = pltpu.VMEM((node_count, 2 * rows, 128), F32)
    by_local = pltpu.VMEM((local_count, 2 * uniques, width), BF16)
    by_local_q = pltpu.VMEM((local_count, 2 * uniques, 128), F32)
    acc = pltpu.VMEM((node_count * 2 * rows, units), F32)
    small = jax.ShapeDtypeStruct((node_count * rows, units), BF16)
    node_sem = [dma((chunks, node_count))] * 2
    local_sem = [dma((chunks, local_count))] * 2
    return pl.pallas_call(
        functools.partial(layer_kernel, node_count, local_count, rows, uniques, chunks),
        out_shape=(
            jax.ShapeDtypeStruct((node_count, 2 * rows, width), BF16),
            small, small, small,
            jax.ShapeDtypeStruct((2 * uniques, width), BF16),
            jax.ShapeDtypeStruct((2 * uniques, 128), F32),
        ),
        in_specs=vmem(2) + [pl.BlockSpec(memory_space=pl.ANY)] * 3,
        out_specs=tuple(vmem(6)),
        scratch_shapes=[
            by_local_q, by_local, by_node,
            pltpu.VMEM(shape, BF16), pltpu.VMEM(shape, BF16),
            pltpu.VMEM(shape, BF16), pltpu.VMEM(shape, BF16),
            pltpu.VMEM((width, units), BF16), pltpu.VMEM((width, units), BF16),
            pltpu.VMEM((units, width), BF16),
            acc, acc, acc,
            by_node, by_node, by_node_q, by_node_q,
            by_local, by_local_q, by_local, by_local_q,
        ] + local_sem + [dma((local_count,))] * 2 + node_sem + node_sem + local_sem
        + [dma((node_count,))] * 2 + [dma((local_count,))] * 2
        + [dma((3,)), dma((2 * chunks,)), dma((3,))],
        compiler_params=pltpu.CompilerParams(
            collective_id=2, has_side_effects=True, vmem_limit_bytes=60 * 2**20),
    )(x, meta, gate, up, down)


def staged(x, meta, w_gate, w_up, w_down, node_count, local_count, rows, uniques):
    owned, width, _ = w_gate.shape
    arrived, zmeta = dispatch(x, meta, node_count, local_count, rows, uniques)

    def by_expert(part):
        part = part.reshape(node_count, local_count, owned, CAP, width)
        return part.transpose(2, 0, 1, 3, 4).reshape(owned, node_count * local_count * CAP, width)

    def by_node(part):
        last = part.shape[-1]
        part = part.reshape(owned, node_count, local_count, CAP, last)
        return part.transpose(1, 2, 0, 3, 4).reshape(node_count, rows, last)

    rows_in = by_expert(arrived[:, :rows])
    grads_in = by_expert(arrived[:, rows:])
    gate_pre = jnp.einsum("erd,edf->erf", rows_in, w_gate, preferred_element_type=F32)
    up_pre = jnp.einsum("erd,edf->erf", rows_in, w_up, preferred_element_type=F32)
    sigmoid_gate = jax.nn.sigmoid(gate_pre)
    activated = gate_pre * sigmoid_gate
    hidden = (activated * up_pre).astype(BF16)
    grad_hidden = jnp.einsum("erd,efd->erf", grads_in, w_down, preferred_element_type=F32)
    grad_gate_pre = (
        grad_hidden * up_pre * sigmoid_gate * (1.0 + gate_pre * (1.0 - sigmoid_gate))
    ).astype(BF16)
    grad_up_pre = (grad_hidden * activated).astype(BF16)
    q_part = jnp.sum(hidden.astype(F32) * grad_hidden, axis=2, keepdims=True)
    partial_out = jnp.einsum("erf,efd->erd", hidden, w_down, preferred_element_type=F32)
    partial_in = jnp.einsum(
        "erf,edf->erd", grad_gate_pre, w_gate, preferred_element_type=F32
    ) + jnp.einsum("erf,edf->erd", grad_up_pre, w_up, preferred_element_type=F32)
    parts = jnp.concatenate(
        [by_node(partial_out.astype(BF16)), by_node(partial_in.astype(BF16))], axis=1)
    q_rows = by_node(jnp.broadcast_to(q_part, q_part.shape[:2] + (128,)))
    q_rows = jnp.concatenate([q_rows, q_rows], axis=1)
    grad_gate = jnp.einsum(
        "erd,erf->edf", rows_in, grad_gate_pre, preferred_element_type=F32).astype(BF16)
    grad_up = jnp.einsum(
        "erd,erf->edf", rows_in, grad_up_pre, preferred_element_type=F32).astype(BF16)
    grad_down = jnp.einsum(
        "erf,erd->efd", hidden, grads_in, preferred_element_type=F32).astype(BF16)

    results, q_unique = combine(parts, q_rows, zmeta, node_count, local_count, rows, uniques)
    return results, q_unique, grad_gate, grad_up, grad_down


def body(tokens, grad_out, router_logits, group_id, expert_ids, w_gate, w_up, w_down):
    owned = w_gate.shape[0]
    node_count = lax.axis_size("node")
    local_count = lax.axis_size("local")
    z = lax.axis_index("local")
    token_count, width = tokens.shape
    expert_total = owned * node_count
    window_groups = expert_total // GSIZE
    slots = owned * CAP
    rows = local_count * slots
    uniques = min(token_count, node_count * slots // 2)

    inside = group_id < window_groups
    chosen = group_id[:, None] * GSIZE + expert_ids
    target = jnp.where(inside[:, None], chosen, expert_total)
    expert_range = jnp.arange(expert_total, dtype=jnp.int32)
    onehot = target[:, :, None] == expert_range[None, None, :]
    per_token = jnp.sum(onehot.astype(F32), axis=1)
    counted = jnp.concatenate([per_token, inside[:, None].astype(F32)], axis=1).astype(BF16)
    order = jnp.arange(token_count, dtype=jnp.int32)
    before = (order[None, :] < order[:, None]).astype(BF16)
    earlier = jnp.dot(before, counted, preferred_element_type=F32)
    slot_rank = jnp.sum(jnp.where(onehot, earlier[:, None, :-1], 0.0), axis=2).astype(jnp.int32)
    unique_rank = earlier[:, -1].astype(jnp.int32)
    picks = (
        (jnp.arange(uniques, dtype=jnp.int32)[:, None] == unique_rank[None, :]) & inside[None, :]
    )
    dest = (target // owned) * (2 * rows) + z * slots + (target % owned) * CAP + slot_rank

    probabilities = jax.nn.softmax(router_logits, axis=-1)
    columns = jnp.arange(router_logits.shape[1], dtype=jnp.int32)
    member = (columns // GSIZE)[None, :] == group_id[:, None]
    mass = jnp.sum(jnp.where(member, probabilities, 0.0), axis=1)
    here = chosen[:, :, None] == columns[None, None, :]
    picked = jnp.sum(jnp.where(here, router_logits[:, None, :], 0.0), axis=2)
    share = jax.nn.softmax(picked, axis=-1)
    weights = jnp.where(inside[:, None], mass[:, None] * share, 0.0)

    pick_bf16 = picks.astype(BF16)
    x = jnp.concatenate(
        [jnp.dot(pick_bf16, tokens, preferred_element_type=F32).astype(BF16),
         jnp.dot(pick_bf16, grad_out, preferred_element_type=F32).astype(BF16)], axis=0)
    facts = jnp.concatenate([dest.astype(F32) + 1.0, weights], axis=1)
    facts = jnp.sum(jnp.where(picks[:, :, None], facts[None], 0.0), axis=1)
    base = facts[:, :2] - 1.0
    moved = jnp.where(base < 0.0, -1.0, base + rows)
    zeros = jnp.zeros((uniques, 1), F32)
    meta = jnp.concatenate(
        [jnp.concatenate([base, facts[:, 2:], zeros], axis=1),
         jnp.concatenate([moved, facts[:, 2:], zeros + 1.0], axis=1)], axis=0)
    meta = jnp.pad(meta, ((0, 0), (0, 123)))

    if owned == 1 and node_count * rows <= 256:
        arrived, hidden, dgate, dup, results, q_unique = layer(
            x, meta, w_gate[0], w_up[0], w_down[0],
            node_count, local_count, rows, uniques, FUSED_CHUNKS)
        over_rows = (((0,), (0,)), ((), ()))
        flat = node_count * rows
        rows_in = arrived[:, :rows].reshape(flat, width)
        grads_in = arrived[:, rows:].reshape(flat, width)

        def outer(left, right):
            return lax.dot_general(
                left, right, over_rows, preferred_element_type=F32).astype(BF16)[None]

        grad_gate, grad_up, grad_down = (
            outer(rows_in, dgate), outer(rows_in, dup), outer(hidden, grads_in))
    else:
        results, q_unique, grad_gate, grad_up, grad_down = staged(
            x, meta, w_gate, w_up, w_down, node_count, local_count, rows, uniques)

    mixed = jnp.einsum("ut,ud->td", pick_bf16, results[:uniques],
                       preferred_element_type=F32).astype(BF16)
    d_tokens = jnp.einsum("ut,ud->td", pick_bf16, results[uniques:],
                          preferred_element_type=F32).astype(BF16)
    q = jnp.sum(jnp.where(picks[:, :, None], q_unique[:uniques, None, :2], 0.0), axis=0)
    q_sum = q[:, 0:1] + q[:, 1:2]
    lean = share[:, 1:2] * q[:, 0:1] - share[:, 0:1] * q[:, 1:2]
    inner = jnp.where(member, router_logits, -jnp.inf)
    inner = jax.nn.softmax(inner, axis=-1)
    tilt = here[:, 0].astype(F32) - here[:, 1].astype(F32)
    d_logits = q_sum * (inner - probabilities) + lean * tilt
    return (mixed, d_tokens, d_logits, grad_gate, grad_up, grad_down)


def solution(mesh):
    rows = P(("node", "local"), None)
    return jax.shard_map(
        body,
        mesh=mesh,
        in_specs=(
            rows, rows, rows, P(("node", "local")), rows,
            P("node", None, "local"), P("node", None, "local"), P("node", "local", None),
        ),
        out_specs=(
            rows, rows, rows,
            P("node", None, "local"), P("node", None, "local"), P("node", "local", None),
        ),
        check_vma=False,
    )
```

```python
import functools

import jax
import jax.numpy as jnp
from jax import lax
from jax.experimental import pallas as pl
from jax.experimental.pallas import tpu as pltpu
from jax.sharding import PartitionSpec as P

GSIZE = 8
CAP = 6
CHUNKS = 4
FUSED_CHUNKS = 8
MESH = pl.DeviceIdType.MESH
F32 = jnp.float32
BF16 = jnp.bfloat16


def greet(n, z, node_count, local_count):
    barrier = pltpu.get_barrier_semaphore()
    for k in range(1, local_count):
        peer = lax.rem(z + k, local_count)
        pl.semaphore_signal(barrier, inc=1, device_id=(n, peer), device_id_type=MESH)
    for k in range(1, node_count):
        peer = lax.rem(n + k, node_count)
        pl.semaphore_signal(barrier, inc=1, device_id=(peer, z), device_id_type=MESH)
    pl.semaphore_wait(barrier, local_count + node_count - 2)


def split(value):
    high = value.astype(BF16)
    return high, (value - high.astype(F32)).astype(BF16)


def one_hots(meta, columns):
    lanes = lax.broadcasted_iota(jnp.int32, (meta.shape[0], columns), 1).astype(F32)
    return lanes == meta[:, 0:1], lanes == meta[:, 1:2]


def dispatch_kernel(
    node_count, local_count, rows, uniques,
    x_ref, meta_ref, out_ref, zmeta_ref,
    zbuf, sendbuf, high_ref, low_ref,
    zsend, zrecv, msend, mrecv, psend, precv, own_sem, place_sem,
):
    n, z = lax.axis_index("node"), lax.axis_index("local")
    width = x_ref.shape[1]
    step = width // CHUNKS
    own = pltpu.make_async_copy(x_ref, zbuf.at[z], own_sem.at[0])
    own.start()
    own_meta = pltpu.make_async_copy(meta_ref, zmeta_ref.at[z], own_sem.at[1])
    own_meta.start()
    greet(n, z, node_count, local_count)
    meta_copies, z_copies = [], []
    for k in range(1, local_count):
        peer = lax.rem(z + k, local_count)
        copy = pltpu.make_async_remote_copy(
            meta_ref, zmeta_ref.at[z], msend.at[k], mrecv.at[k],
            device_id=(n, peer), device_id_type=MESH)
        copy.start()
        meta_copies.append(copy)
    for c in range(CHUNKS):
        cols = pl.ds(c * step, step)
        for k in range(1, local_count):
            peer = lax.rem(z + k, local_count)
            copy = pltpu.make_async_remote_copy(
                x_ref.at[:, cols], zbuf.at[z, :, cols], zsend.at[c, k], zrecv.at[c, k],
                device_id=(n, peer), device_id_type=MESH)
            copy.start()
            z_copies.append(copy)
    own.wait()
    own_meta.wait()
    for copy in meta_copies:
        copy.wait()
    meta = zmeta_ref[...].reshape(local_count * 2 * uniques, 128)
    hot0, hot1 = one_hots(meta, node_count * 2 * rows)
    is_grad = meta[:, 4:5] > 0.5
    scale0 = jnp.where(is_grad, meta[:, 2:3], 1.0)
    scale1 = jnp.where(is_grad, meta[:, 3:4], 1.0)
    mix = jnp.where(hot0, scale0, 0.0) + jnp.where(hot1, scale1, 0.0)
    high, low = split(mix)
    high_ref[...] = high
    low_ref[...] = low
    p_copies, places = [], []
    for c in range(CHUNKS):
        cols = pl.ds(c * step, step)
        for k in range(1, local_count):
            z_copies[c * (local_count - 1) + k - 1].wait()
        block = zbuf[:, :, cols].reshape(local_count * 2 * uniques, step)
        contract = (((0,), (0,)), ((), ()))
        picked = lax.dot_general(
            high_ref[...], block, contract, preferred_element_type=F32
        ) + lax.dot_general(low_ref[...], block, contract, preferred_element_type=F32)
        sendbuf[:, :, cols] = picked.astype(BF16).reshape(node_count, 2 * rows, step)
        for k in range(1, node_count):
            peer = lax.rem(n + k, node_count)
            copy = pltpu.make_async_remote_copy(
                sendbuf.at[peer, :, cols], out_ref.at[n, :, cols],
                psend.at[c, k], precv.at[c, k],
                device_id=(peer, z), device_id_type=MESH)
            copy.start()
            p_copies.append(copy)
        place = pltpu.make_async_copy(
            sendbuf.at[n, :, cols], out_ref.at[n, :, cols], place_sem.at[c])
        place.start()
        places.append(place)
    for copy in places + p_copies:
        copy.wait()


def combine_kernel(
    node_count, local_count, rows, uniques,
    part_ref, q_ref, zmeta_ref, out_ref, qout_ref,
    pbuf, qbuf, sendbuf, qsend, rbuf, rqbuf, high_ref, low_ref,
    psend, precv, qpsend, qprecv, zsend, zrecv, qzsend, qzrecv, own_sem,
):
    n, z = lax.axis_index("node"), lax.axis_index("local")
    width = part_ref.shape[2]
    step = width // CHUNKS
    own = pltpu.make_async_copy(part_ref.at[n], pbuf.at[n], own_sem.at[0])
    own.start()
    own_q = pltpu.make_async_copy(q_ref.at[n], qbuf.at[n], own_sem.at[1])
    own_q.start()
    greet(n, z, node_count, local_count)
    p_copies, q_copies = [], []
    for k in range(1, node_count):
        peer = lax.rem(n + k, node_count)
        copy = pltpu.make_async_remote_copy(
            q_ref.at[peer], qbuf.at[n], qpsend.at[k], qprecv.at[k],
            device_id=(peer, z), device_id_type=MESH)
        copy.start()
        q_copies.append(copy)
    for c in range(CHUNKS):
        cols = pl.ds(c * step, step)
        for k in range(1, node_count):
            peer = lax.rem(n + k, node_count)
            copy = pltpu.make_async_remote_copy(
                part_ref.at[peer, :, cols], pbuf.at[n, :, cols],
                psend.at[c, k], precv.at[c, k],
                device_id=(peer, z), device_id_type=MESH)
            copy.start()
            p_copies.append(copy)
    meta = zmeta_ref[...].reshape(local_count * 2 * uniques, 128)
    hot0, hot1 = one_hots(meta, node_count * 2 * rows)
    is_grad = meta[:, 4:5] > 0.5
    scale0 = jnp.where(is_grad, 1.0, meta[:, 2:3])
    scale1 = jnp.where(is_grad, 1.0, meta[:, 3:4])
    mix = jnp.where(hot0, scale0, 0.0) + jnp.where(hot1, scale1, 0.0)
    high, low = split(mix)
    high_ref[...] = high
    low_ref[...] = low
    own.wait()
    own_q.wait()
    for copy in q_copies:
        copy.wait()
    q_all = qbuf[...].reshape(node_count * 2 * rows, 128)
    q0 = jnp.dot(jnp.where(hot0, 1.0, 0.0), q_all, preferred_element_type=F32,
                 precision=lax.Precision.HIGHEST)
    q1 = jnp.dot(jnp.where(hot1, 1.0, 0.0), q_all, preferred_element_type=F32,
                 precision=lax.Precision.HIGHEST)
    lane = lax.broadcasted_iota(jnp.int32, q0.shape, 1)
    qsend[...] = jnp.where(lane == 0, q0, q1).reshape(local_count, 2 * uniques, 128)
    z_copies, qz_copies = [], []
    for c in range(CHUNKS):
        cols = pl.ds(c * step, step)
        for k in range(1, node_count):
            p_copies[c * (node_count - 1) + k - 1].wait()
        block = pbuf[:, :, cols].reshape(node_count * 2 * rows, step)
        summed = jnp.dot(high_ref[...], block, preferred_element_type=F32) + jnp.dot(
            low_ref[...], block, preferred_element_type=F32)
        sendbuf[:, :, cols] = summed.astype(BF16).reshape(local_count, 2 * uniques, step)
        for k in range(1, local_count):
            peer = lax.rem(z + k, local_count)
            copy = pltpu.make_async_remote_copy(
                sendbuf.at[peer, :, cols], rbuf.at[k, :, cols],
                zsend.at[c, k], zrecv.at[c, k],
                device_id=(n, peer), device_id_type=MESH)
            copy.start()
            z_copies.append(copy)
            if c == 0:
                copy = pltpu.make_async_remote_copy(
                    qsend.at[peer], rqbuf.at[k], qzsend.at[k], qzrecv.at[k],
                    device_id=(n, peer), device_id_type=MESH)
                copy.start()
                qz_copies.append(copy)
    for copy in qz_copies:
        copy.wait()
    q_total = qsend[z]
    for k in range(1, local_count):
        q_total = q_total + rqbuf[k]
    qout_ref[...] = q_total
    for c in range(CHUNKS):
        cols = pl.ds(c * step, step)
        for k in range(1, local_count):
            z_copies[c * (local_count - 1) + k - 1].wait()
        total = sendbuf[z, :, cols].astype(F32)
        for k in range(1, local_count):
            total = total + rbuf[k, :, cols].astype(F32)
        out_ref[:, cols] = total.astype(BF16)


def vmem(count):
    return [pl.BlockSpec(memory_space=pltpu.VMEM)] * count


def dispatch(x, meta, node_count, local_count, rows, uniques):
    width = x.shape[1]
    dma = pltpu.SemaphoreType.DMA
    shape = (local_count * 2 * uniques, node_count * 2 * rows)
    return pl.pallas_call(
        functools.partial(dispatch_kernel, node_count, local_count, rows, uniques),
        out_shape=(
            jax.ShapeDtypeStruct((node_count, 2 * rows, width), BF16),
            jax.ShapeDtypeStruct((local_count, 2 * uniques, 128), F32),
        ),
        in_specs=vmem(2),
        out_specs=tuple(vmem(2)),
        scratch_shapes=[
            pltpu.VMEM((local_count, 2 * uniques, width), BF16),
            pltpu.VMEM((node_count, 2 * rows, width), BF16),
            pltpu.VMEM(shape, BF16),
            pltpu.VMEM(shape, BF16),
            dma((CHUNKS, local_count)), dma((CHUNKS, local_count)),
            dma((local_count,)), dma((local_count,)),
            dma((CHUNKS, node_count)), dma((CHUNKS, node_count)),
            dma((2,)), dma((CHUNKS,)),
        ],
        compiler_params=pltpu.CompilerParams(
            collective_id=0, has_side_effects=True, vmem_limit_bytes=60 * 2**20),
    )(x, meta)


def combine(parts, q_rows, zmeta, node_count, local_count, rows, uniques):
    width = parts.shape[2]
    dma = pltpu.SemaphoreType.DMA
    shape = (local_count * 2 * uniques, node_count * 2 * rows)
    return pl.pallas_call(
        functools.partial(combine_kernel, node_count, local_count, rows, uniques),
        out_shape=(
            jax.ShapeDtypeStruct((2 * uniques, width), BF16),
            jax.ShapeDtypeStruct((2 * uniques, 128), F32),
        ),
        in_specs=vmem(3),
        out_specs=tuple(vmem(2)),
        scratch_shapes=[
            pltpu.VMEM((node_count, 2 * rows, width), BF16),
            pltpu.VMEM((node_count, 2 * rows, 128), F32),
            pltpu.VMEM((local_count, 2 * uniques, width), BF16),
            pltpu.VMEM((local_count, 2 * uniques, 128), F32),
            pltpu.VMEM((local_count, 2 * uniques, width), BF16),
            pltpu.VMEM((local_count, 2 * uniques, 128), F32),
            pltpu.VMEM(shape, BF16),
            pltpu.VMEM(shape, BF16),
            dma((CHUNKS, node_count)), dma((CHUNKS, node_count)),
            dma((node_count,)), dma((node_count,)),
            dma((CHUNKS, local_count)), dma((CHUNKS, local_count)),
            dma((local_count,)), dma((local_count,)),
            dma((2,)),
        ],
        compiler_params=pltpu.CompilerParams(
            collective_id=1, has_side_effects=True, vmem_limit_bytes=60 * 2**20),
    )(parts, q_rows, zmeta)


def layer_kernel(
    node_count, local_count, rows, uniques, chunks,
    x_ref, meta_ref, gate_hbm, up_hbm, down_hbm,
    out_ref, qout_ref, ggate_hbm, gup_hbm, gdown_hbm,
    arrived_ref, hidden_ref, dgate_ref, dup_ref, ggate_ref, gup_ref, gdown_ref, grad_sem,
    zmeta, zbuf, sendbuf, high_ref, low_ref, back_high, back_low,
    gate_ref, up_ref, down_ref, gate_acc, up_acc, down_acc,
    parts, pbuf, q_rows, qbuf, sums, qsums, rbuf, rqbuf,
    zsend, zrecv, msend, mrecv, psend, precv, psend2, precv2, zsend2, zrecv2,
    qsend, qrecv, qsend2, qrecv2, own_sem, place_sem, weight_sem,
):
    n, z = lax.axis_index("node"), lax.axis_index("local")
    width = x_ref.shape[1]
    step = width // chunks
    total_rows = node_count * 2 * rows
    total_uniques = local_count * 2 * uniques

    def cols(c):
        return pl.ds(pl.multiple_of(c * step, step), step)

    def remote(src, dst, send, recv, device):
        return pltpu.make_async_remote_copy(
            src, dst, send, recv, device_id=device, device_id_type=MESH)

    def z_peer(k):
        return lax.rem(z + k, local_count)

    def n_peer(k):
        return lax.rem(n + k, node_count)

    def z_copy(c, k):
        return remote(x_ref.at[:, cols(c)], zbuf.at[z, :, cols(c)],
                      zsend.at[c, k], zrecv.at[c, k], (n, z_peer(k)))

    def p_copy(c, k):
        return remote(sendbuf.at[n_peer(k), :, cols(c)], arrived_ref.at[n, :, cols(c)],
                      psend.at[c, k], precv.at[c, k], (n_peer(k), z))

    def place(c):
        return pltpu.make_async_copy(
            sendbuf.at[n, :, cols(c)], arrived_ref.at[n, :, cols(c)], place_sem.at[c])

    def p_copy2(c, k):
        return remote(parts.at[n_peer(k), :, cols(c)], pbuf.at[n, :, cols(c)],
                      psend2.at[c, k], precv2.at[c, k], (n_peer(k), z))

    def place2(c):
        return pltpu.make_async_copy(
            parts.at[n, :, cols(c)], pbuf.at[n, :, cols(c)], place_sem.at[chunks + c])

    def z_copy2(c, k):
        return remote(sums.at[z_peer(k), :, cols(c)], rbuf.at[k, :, cols(c)],
                      zsend2.at[c, k], zrecv2.at[c, k], (n, z_peer(k)))

    weights = [
        pltpu.make_async_copy(gate_hbm, gate_ref, weight_sem.at[0]),
        pltpu.make_async_copy(up_hbm, up_ref, weight_sem.at[1]),
        pltpu.make_async_copy(down_hbm, down_ref, weight_sem.at[2]),
    ]
    own = pltpu.make_async_copy(x_ref, zbuf.at[z], own_sem.at[0])
    own.start()
    own_meta = pltpu.make_async_copy(meta_ref, zmeta.at[z], own_sem.at[1])
    own_meta.start()
    greet(n, z, node_count, local_count)
    meta_copies = [
        remote(meta_ref, zmeta.at[z], msend.at[k], mrecv.at[k], (n, z_peer(k)))
        for k in range(1, local_count)
    ]
    for copy in meta_copies:
        copy.start()

    @pl.loop(0, chunks)
    def _(c):
        for k in range(1, local_count):
            z_copy(c, k).start()

    for copy in weights:
        copy.start()
    gate_acc[...] = jnp.zeros_like(gate_acc)
    up_acc[...] = jnp.zeros_like(up_acc)
    down_acc[...] = jnp.zeros_like(down_acc)
    own.wait()
    own_meta.wait()
    for copy in meta_copies:
        copy.wait()
    meta = zmeta[...].reshape(total_uniques, 128)
    hot0, hot1 = one_hots(meta, total_rows)
    is_grad = meta[:, 4:5] > 0.5
    w0, w1 = meta[:, 2:3], meta[:, 3:4]
    mix = jnp.where(hot0, jnp.where(is_grad, w0, 1.0), 0.0) + jnp.where(
        hot1, jnp.where(is_grad, w1, 1.0), 0.0)
    high_ref[...], low_ref[...] = split(mix)
    mix = jnp.where(hot0, jnp.where(is_grad, 1.0, w0), 0.0) + jnp.where(
        hot1, jnp.where(is_grad, 1.0, w1), 0.0)
    back_high[...], back_low[...] = split(mix)
    over_rows = (((0,), (0,)), ((), ()))
    over_last = (((1,), (1,)), ((), ()))

    def gather(c):
        for k in range(1, node_count):
            p_copy(c, k).wait()
        place(c).wait()
        block = arrived_ref[:, :, cols(c)].reshape(total_rows, step)
        gate_acc[...] += jnp.dot(block, gate_ref[cols(c), :], preferred_element_type=F32)
        up_acc[...] += jnp.dot(block, up_ref[cols(c), :], preferred_element_type=F32)
        down_acc[...] += lax.dot_general(
            block, down_ref[:, cols(c)], over_last, preferred_element_type=F32)

    @pl.loop(0, chunks)
    def _(c):
        for k in range(1, local_count):
            z_copy(c, k).wait()
        block = zbuf[:, :, cols(c)].reshape(total_uniques, step)
        picked = lax.dot_general(
            high_ref[...], block, over_rows, preferred_element_type=F32
        ) + lax.dot_general(low_ref[...], block, over_rows, preferred_element_type=F32)
        sendbuf[:, :, cols(c)] = picked.astype(BF16).reshape(node_count, 2 * rows, step)
        for k in range(1, node_count):
            p_copy(c, k).start()
        place(c).start()

        @pl.when(c == 0)
        def _():
            for copy in weights:
                copy.wait()

        @pl.when(c > 0)
        def _():
            gather(c - 1)

    gather(chunks - 1)

    hidden_units = gate_acc.shape[1]

    def half(acc, kind):
        whole = acc[...].reshape(node_count, 2 * rows, hidden_units)
        return whole[:, kind * rows:(kind + 1) * rows].reshape(node_count * rows, hidden_units)

    gate_pre, up_pre, grad_hidden = half(gate_acc, 0), half(up_acc, 0), half(down_acc, 1)
    sigmoid_gate = jax.nn.sigmoid(gate_pre)
    activated = gate_pre * sigmoid_gate
    hidden = (activated * up_pre).astype(BF16)
    hidden_ref[...] = hidden
    dgate_ref[...] = (
        grad_hidden * up_pre * sigmoid_gate * (1.0 + gate_pre * (1.0 - sigmoid_gate))
    ).astype(BF16)
    dup_ref[...] = (grad_hidden * activated).astype(BF16)
    q_part = jnp.sum(hidden.astype(F32) * grad_hidden, axis=1, keepdims=True)
    q_part = jnp.broadcast_to(q_part, (node_count * rows, 128)).reshape(node_count, rows, 128)
    q_rows[...] = jnp.concatenate([q_part, q_part], axis=1)

    def return_sums(c):
        for k in range(1, node_count):
            p_copy2(c, k).wait()
        place2(c).wait()
        block = pbuf[:, :, cols(c)].reshape(total_rows, step)
        summed = jnp.dot(back_high[...], block, preferred_element_type=F32) + jnp.dot(
            back_low[...], block, preferred_element_type=F32)
        sums[:, :, cols(c)] = summed.astype(BF16).reshape(local_count, 2 * uniques, step)
        for k in range(1, local_count):
            z_copy2(c, k).start()

    def grad_copies(c):
        return [
            pltpu.make_async_copy(
                ggate_ref.at[cols(c), :], ggate_hbm.at[cols(c), :], grad_sem.at[0, c]),
            pltpu.make_async_copy(
                gup_ref.at[cols(c), :], gup_hbm.at[cols(c), :], grad_sem.at[1, c]),
            pltpu.make_async_copy(
                gdown_ref.at[:, cols(c)], gdown_hbm.at[:, cols(c)], grad_sem.at[2, c]),
        ]

    def weight_grads(c):
        block = arrived_ref[:, :, cols(c)].astype(F32)
        rows_in = block[:, :rows].reshape(node_count * rows, step).astype(BF16)
        grads_in = block[:, rows:].reshape(node_count * rows, step).astype(BF16)
        ggate_ref[cols(c), :] = lax.dot_general(
            rows_in, dgate_ref[...], over_rows, preferred_element_type=F32).astype(BF16)
        gup_ref[cols(c), :] = lax.dot_general(
            rows_in, dup_ref[...], over_rows, preferred_element_type=F32).astype(BF16)
        gdown_ref[:, cols(c)] = lax.dot_general(
            hidden_ref[...], grads_in, over_rows, preferred_element_type=F32).astype(BF16)
        for copy in grad_copies(c):
            copy.start()

    @pl.loop(0, chunks)
    def _(c):
        part_out = jnp.dot(hidden_ref[...], down_ref[:, cols(c)], preferred_element_type=F32)
        part_in = lax.dot_general(
            dgate_ref[...], gate_ref[cols(c), :], over_last, preferred_element_type=F32
        ) + lax.dot_general(
            dup_ref[...], up_ref[cols(c), :], over_last, preferred_element_type=F32)
        both = jnp.concatenate(
            [part_out.reshape(node_count, rows, step), part_in.reshape(node_count, rows, step)],
            axis=1)
        parts[:, :, cols(c)] = both.astype(BF16)
        for k in range(1, node_count):
            p_copy2(c, k).start()
        place2(c).start()

        @pl.when(c > 0)
        def _():
            return_sums(c - 1)

        weight_grads(c)

    q_own = pltpu.make_async_copy(q_rows.at[n], qbuf.at[n], own_sem.at[2])
    q_own.start()
    q_copies = [
        remote(q_rows.at[n_peer(k)], qbuf.at[n], qsend.at[k], qrecv.at[k], (n_peer(k), z))
        for k in range(1, node_count)
    ]
    for copy in q_copies:
        copy.start()
    return_sums(chunks - 1)
    q_own.wait()
    for copy in q_copies:
        copy.wait()
    meta = zmeta[...].reshape(total_uniques, 128)
    hot0, hot1 = one_hots(meta, total_rows)
    q_all = qbuf[...].reshape(total_rows, 128)
    q0 = jnp.dot(jnp.where(hot0, 1.0, 0.0), q_all, preferred_element_type=F32,
                 precision=lax.Precision.HIGHEST)
    q1 = jnp.dot(jnp.where(hot1, 1.0, 0.0), q_all, preferred_element_type=F32,
                 precision=lax.Precision.HIGHEST)
    lane = lax.broadcasted_iota(jnp.int32, q0.shape, 1)
    qsums[...] = jnp.where(lane == 0, q0, q1).reshape(local_count, 2 * uniques, 128)
    q_copies = [
        remote(qsums.at[z_peer(k)], rqbuf.at[k], qsend2.at[k], qrecv2.at[k], (n, z_peer(k)))
        for k in range(1, local_count)
    ]
    for copy in q_copies:
        copy.start()

    @pl.loop(0, chunks)
    def _(c):
        for k in range(1, local_count):
            z_copy2(c, k).wait()
        total = sums[z, :, cols(c)].astype(F32)
        for k in range(1, local_count):
            total = total + rbuf[k, :, cols(c)].astype(F32)
        out_ref[:, cols(c)] = total.astype(BF16)

    for copy in q_copies:
        copy.wait()
    q_total = qsums[z]
    for k in range(1, local_count):
        q_total = q_total + rqbuf[k]
    qout_ref[...] = q_total

    @pl.loop(0, chunks)
    def _(c):
        for copy in grad_copies(c):
            copy.wait()


def layer(x, meta, gate, up, down, node_count, local_count, rows, uniques, chunks):
    width, units = gate.shape
    dma = pltpu.SemaphoreType.DMA
    shape = (local_count * 2 * uniques, node_count * 2 * rows)
    by_node = pltpu.VMEM((node_count, 2 * rows, width), BF16)
    by_node_q = pltpu.VMEM((node_count, 2 * rows, 128), F32)
    by_local = pltpu.VMEM((local_count, 2 * uniques, width), BF16)
    by_local_q = pltpu.VMEM((local_count, 2 * uniques, 128), F32)
    acc = pltpu.VMEM((node_count * 2 * rows, units), F32)
    small = pltpu.VMEM((node_count * rows, units), BF16)
    node_sem = [dma((chunks, node_count))] * 2
    local_sem = [dma((chunks, local_count))] * 2
    return pl.pallas_call(
        functools.partial(layer_kernel, node_count, local_count, rows, uniques, chunks),
        out_shape=(
            jax.ShapeDtypeStruct((2 * uniques, width), BF16),
            jax.ShapeDtypeStruct((2 * uniques, 128), F32),
            jax.ShapeDtypeStruct((width, units), BF16),
            jax.ShapeDtypeStruct((width, units), BF16),
            jax.ShapeDtypeStruct((units, width), BF16),
        ),
        in_specs=vmem(2) + [pl.BlockSpec(memory_space=pl.ANY)] * 3,
        out_specs=tuple(vmem(2) + [pl.BlockSpec(memory_space=pl.ANY)] * 3),
        scratch_shapes=[
            by_node, small, small, small,
            pltpu.VMEM((width, units), BF16), pltpu.VMEM((width, units), BF16),
            pltpu.VMEM((units, width), BF16), dma((3, chunks)),
            by_local_q, by_local, by_node,
            pltpu.VMEM(shape, BF16), pltpu.VMEM(shape, BF16),
            pltpu.VMEM(shape, BF16), pltpu.VMEM(shape, BF16),
            pltpu.VMEM((width, units), BF16), pltpu.VMEM((width, units), BF16),
            pltpu.VMEM((units, width), BF16),
            acc, acc, acc,
            by_node, by_node, by_node_q, by_node_q,
            by_local, by_local_q, by_local, by_local_q,
        ] + local_sem + [dma((local_count,))] * 2 + node_sem + node_sem + local_sem
        + [dma((node_count,))] * 2 + [dma((local_count,))] * 2
        + [dma((3,)), dma((2 * chunks,)), dma((3,))],
        compiler_params=pltpu.CompilerParams(
            collective_id=2, has_side_effects=True, vmem_limit_bytes=60 * 2**20),
    )(x, meta, gate, up, down)


def staged(x, meta, w_gate, w_up, w_down, node_count, local_count, rows, uniques):
    owned, width, _ = w_gate.shape
    arrived, zmeta = dispatch(x, meta, node_count, local_count, rows, uniques)

    def by_expert(part):
        part = part.reshape(node_count, local_count, owned, CAP, width)
        return part.transpose(2, 0, 1, 3, 4).reshape(owned, node_count * local_count * CAP, width)

    def by_node(part):
        last = part.shape[-1]
        part = part.reshape(owned, node_count, local_count, CAP, last)
        return part.transpose(1, 2, 0, 3, 4).reshape(node_count, rows, last)

    rows_in = by_expert(arrived[:, :rows])
    grads_in = by_expert(arrived[:, rows:])
    gate_pre = jnp.einsum("erd,edf->erf", rows_in, w_gate, preferred_element_type=F32)
    up_pre = jnp.einsum("erd,edf->erf", rows_in, w_up, preferred_element_type=F32)
    sigmoid_gate = jax.nn.sigmoid(gate_pre)
    activated = gate_pre * sigmoid_gate
    hidden = (activated * up_pre).astype(BF16)
    grad_hidden = jnp.einsum("erd,efd->erf", grads_in, w_down, preferred_element_type=F32)
    grad_gate_pre = (
        grad_hidden * up_pre * sigmoid_gate * (1.0 + gate_pre * (1.0 - sigmoid_gate))
    ).astype(BF16)
    grad_up_pre = (grad_hidden * activated).astype(BF16)
    q_part = jnp.sum(hidden.astype(F32) * grad_hidden, axis=2, keepdims=True)
    partial_out = jnp.einsum("erf,efd->erd", hidden, w_down, preferred_element_type=F32)
    partial_in = jnp.einsum(
        "erf,edf->erd", grad_gate_pre, w_gate, preferred_element_type=F32
    ) + jnp.einsum("erf,edf->erd", grad_up_pre, w_up, preferred_element_type=F32)
    parts = jnp.concatenate(
        [by_node(partial_out.astype(BF16)), by_node(partial_in.astype(BF16))], axis=1)
    q_rows = by_node(jnp.broadcast_to(q_part, q_part.shape[:2] + (128,)))
    q_rows = jnp.concatenate([q_rows, q_rows], axis=1)
    grad_gate = jnp.einsum(
        "erd,erf->edf", rows_in, grad_gate_pre, preferred_element_type=F32).astype(BF16)
    grad_up = jnp.einsum(
        "erd,erf->edf", rows_in, grad_up_pre, preferred_element_type=F32).astype(BF16)
    grad_down = jnp.einsum(
        "erf,erd->efd", hidden, grads_in, preferred_element_type=F32).astype(BF16)

    results, q_unique = combine(parts, q_rows, zmeta, node_count, local_count, rows, uniques)
    return results, q_unique, grad_gate, grad_up, grad_down


def body(tokens, grad_out, router_logits, group_id, expert_ids, w_gate, w_up, w_down):
    owned = w_gate.shape[0]
    node_count = lax.axis_size("node")
    local_count = lax.axis_size("local")
    z = lax.axis_index("local")
    token_count, width = tokens.shape
    expert_total = owned * node_count
    window_groups = expert_total // GSIZE
    slots = owned * CAP
    rows = local_count * slots
    uniques = min(token_count, node_count * slots // 2)

    inside = group_id < window_groups
    chosen = group_id[:, None] * GSIZE + expert_ids
    target = jnp.where(inside[:, None], chosen, expert_total)
    expert_range = jnp.arange(expert_total, dtype=jnp.int32)
    onehot = target[:, :, None] == expert_range[None, None, :]
    per_token = jnp.sum(onehot.astype(F32), axis=1)
    counted = jnp.concatenate([per_token, inside[:, None].astype(F32)], axis=1).astype(BF16)
    order = jnp.arange(token_count, dtype=jnp.int32)
    before = (order[None, :] < order[:, None]).astype(BF16)
    earlier = jnp.dot(before, counted, preferred_element_type=F32)
    slot_rank = jnp.sum(jnp.where(onehot, earlier[:, None, :-1], 0.0), axis=2).astype(jnp.int32)
    unique_rank = earlier[:, -1].astype(jnp.int32)
    picks = (
        (jnp.arange(uniques, dtype=jnp.int32)[:, None] == unique_rank[None, :]) & inside[None, :]
    )
    dest = (target // owned) * (2 * rows) + z * slots + (target % owned) * CAP + slot_rank

    probabilities = jax.nn.softmax(router_logits, axis=-1)
    columns = jnp.arange(router_logits.shape[1], dtype=jnp.int32)
    member = (columns // GSIZE)[None, :] == group_id[:, None]
    mass = jnp.sum(jnp.where(member, probabilities, 0.0), axis=1)
    here = chosen[:, :, None] == columns[None, None, :]
    picked = jnp.sum(jnp.where(here, router_logits[:, None, :], 0.0), axis=2)
    share = jax.nn.softmax(picked, axis=-1)
    weights = jnp.where(inside[:, None], mass[:, None] * share, 0.0)

    pick_bf16 = picks.astype(BF16)
    x = jnp.concatenate(
        [jnp.dot(pick_bf16, tokens, preferred_element_type=F32).astype(BF16),
         jnp.dot(pick_bf16, grad_out, preferred_element_type=F32).astype(BF16)], axis=0)
    facts = jnp.concatenate([dest.astype(F32) + 1.0, weights], axis=1)
    facts = jnp.sum(jnp.where(picks[:, :, None], facts[None], 0.0), axis=1)
    base = facts[:, :2] - 1.0
    moved = jnp.where(base < 0.0, -1.0, base + rows)
    zeros = jnp.zeros((uniques, 1), F32)
    meta = jnp.concatenate(
        [jnp.concatenate([base, facts[:, 2:], zeros], axis=1),
         jnp.concatenate([moved, facts[:, 2:], zeros + 1.0], axis=1)], axis=0)
    meta = jnp.pad(meta, ((0, 0), (0, 123)))

    if owned == 1 and node_count * rows <= 256:
        results, q_unique, grad_gate, grad_up, grad_down = layer(
            x, meta, w_gate[0], w_up[0], w_down[0],
            node_count, local_count, rows, uniques, FUSED_CHUNKS)
        grad_gate, grad_up, grad_down = grad_gate[None], grad_up[None], grad_down[None]
    else:
        results, q_unique, grad_gate, grad_up, grad_down = staged(
            x, meta, w_gate, w_up, w_down, node_count, local_count, rows, uniques)

    mixed = jnp.einsum("ut,ud->td", pick_bf16, results[:uniques],
                       preferred_element_type=F32).astype(BF16)
    d_tokens = jnp.einsum("ut,ud->td", pick_bf16, results[uniques:],
                          preferred_element_type=F32).astype(BF16)
    q = jnp.sum(jnp.where(picks[:, :, None], q_unique[:uniques, None, :2], 0.0), axis=0)
    q_sum = q[:, 0:1] + q[:, 1:2]
    lean = share[:, 1:2] * q[:, 0:1] - share[:, 0:1] * q[:, 1:2]
    inner = jnp.where(member, router_logits, -jnp.inf)
    inner = jax.nn.softmax(inner, axis=-1)
    tilt = here[:, 0].astype(F32) - here[:, 1].astype(F32)
    d_logits = q_sum * (inner - probabilities) + lean * tilt
    return (mixed, d_tokens, d_logits, grad_gate, grad_up, grad_down)


def solution(mesh):
    rows = P(("node", "local"), None)
    return jax.shard_map(
        body,
        mesh=mesh,
        in_specs=(
            rows, rows, rows, P(("node", "local")), rows,
            P("node", None, "local"), P("node", None, "local"), P("node", "local", None),
        ),
        out_specs=(
            rows, rows, rows,
            P("node", None, "local"), P("node", None, "local"), P("node", "local", None),
        ),
        check_vma=False,
    )
```
